32 devices in a mesh: dp: 16 (over z, x, core), depth: 2 (over y).
Axes of the slice: x: 2, y: 2, z: 4, core: 2. Of those that a mesh axis runs over, the one named last changes fastest.
Arguments:
- volume: bfloat16 [16, 4, 4, 8, 128], P('dp', None, 'depth'), may hold values from -6 to 6
- kernel_one: bfloat16 [32, 4, 3, 3, 3], replicated, may hold values from -0.625 to 0.625
- bias_one: float32 [32], replicated, may hold values from -0.5 to 0.5
- kernel_two: bfloat16 [64, 32, 3, 3, 3], replicated, may hold values from -0.21875 to 0.21875
- bias_two: float32 [64], replicated, may hold values from -0.5 to 0.5
- cotangent: bfloat16 [16, 64, 4, 8, 128], P('dp', None, 'depth'), may hold values from -0.0234375 to 0.0234375
Outputs:
- features: bfloat16 [16, 64, 4, 8, 128], P('dp', None, 'depth')
- grad_kernel_one: float32 [32, 4, 3, 3, 3], replicated
- grad_bias_one: float32 [32], replicated
- grad_kernel_two: float32 [64, 32, 3, 3, 3], replicated
- grad_bias_two: float32 [64], replicated
The draws below stay inside these ranges and needn't reach their ends.
All inputs are finite; a program needn't handle non-finite values.
Results may differ from the reference program's by a relative error of at most 0.006.
Values may be sent and summed in bfloat16 or wider, within the bound.
A program may use at most 64 MiB of HBM per device.

```python
import jax
import jax.numpy as jnp
from jax import lax

C_IN = 4
C_ONE = 32
C_TWO = 64
HY = 8
HX = 128
SAMPLES = 16
NZ = 4


def level_of(rng, shape, shards, least, high):
    def one(position, blocks):
        steps = jax.random.uniform(jax.random.fold_in(jax.random.fold_in(rng, 6), position), (blocks,), jnp.float32, least / len(shards), high / len(shards))
        return jnp.repeat(jnp.exp(steps), shape[position] // blocks).reshape((-1,) + (1,) * (len(shape) - position - 1))

    level = one(*shards[0])
    for cut in shards[1:]:
        level = level * one(*cut)
    return level


def noise(stream_key, shape, scale, bound, shards=(), held_as=jnp.bfloat16):
    drawn = jax.random.normal(stream_key, shape, jnp.float32) * scale
    if len(shards) > 0:
        drawn = level_of(stream_key, shape, shards, -0.22, 0.18) * drawn
    return jnp.clip(drawn, min=-bound, max=bound).astype(held_as)


def setup_inputs(seed: int = 0) -> dict:
    streams_of = jax.random.split(jax.random.key(seed), 7)
    return {
        "volume": noise(streams_of[0], (SAMPLES, C_IN, NZ, HY, HX), 1.0, 6.0, ((0, 16), (2, 2))),
        "kernel_one": noise(streams_of[1], (C_ONE, C_IN, 3, 3, 3), (27 * C_IN) ** -0.5, 0.625),
        "bias_one": jnp.clip(jax.random.uniform(streams_of[2], (C_ONE,), jnp.float32, -0.5, 0.5), -0.5, 0.5),
        "kernel_two": noise(streams_of[3], (C_TWO, C_ONE, 3, 3, 3), (27 * C_ONE) ** -0.5, 0.21875),
        "bias_two": jnp.clip(jax.random.uniform(streams_of[4], (C_TWO,), jnp.float32, -0.5, 0.5), -0.5, 0.5),
        "cotangent": noise(streams_of[5], (SAMPLES, C_TWO, NZ, HY, HX), (1.0 / (SAMPLES * NZ * HY * HX) ** 0.5), 0.0234375, ((0, 16), (2, 2))),
    }


FORWARD_DIMS = ('NCDHW', 'OIDHW', 'NCDHW')
KERNEL_DIMS = ('CNDHW', 'IODHW', 'CNDHW')

def convolve(inputs, kernel):
    return lax.conv_general_dilated(inputs.astype(jnp.float32), kernel.astype(jnp.float32), (1, 1, 1), ((1, 1), (1, 1), (1, 1)), dimension_numbers=FORWARD_DIMS, precision=lax.Precision.HIGHEST)

def kernel_grad(inputs, slope):
    return lax.conv_general_dilated(inputs.astype(jnp.float32), slope.astype(jnp.float32), (1, 1, 1), ((1, 1), (1, 1), (1, 1)), dimension_numbers=KERNEL_DIMS, precision=lax.Precision.HIGHEST)

def silu_slope(value):
    sig = jax.nn.sigmoid(value)
    return sig * (1.0 + value * (1.0 - sig))

def reference(volume, kernel_one, bias_one, kernel_two, bias_two, cotangent):
    flipped = jnp.transpose(jnp.flip(kernel_two, (2, 3, 4)), (1, 0, 2, 3, 4))

    def one_sample(carry, pieces):
        sample, upstream = pieces
        sample = sample[None]
        upstream = upstream[None]
        pre_one = convolve(sample, kernel_one) + bias_one[None, :, None, None, None]
        act_one = jax.nn.silu(pre_one).astype(jnp.bfloat16)
        pre_two = convolve(act_one, kernel_two) + bias_two[None, :, None, None, None]
        feature = jax.nn.silu(pre_two).astype(jnp.bfloat16)
        slope_two = (upstream.astype(jnp.float32) * silu_slope(pre_two)).astype(jnp.bfloat16)
        grad_two = kernel_grad(act_one, slope_two)
        bias_grad_two = lax.optimization_barrier(jnp.sum(slope_two.astype(jnp.float32), axis=(0, 2, 3, 4)))
        back_one = convolve(slope_two, flipped)
        slope_one = (back_one * silu_slope(pre_one)).astype(jnp.bfloat16)
        grad_one = kernel_grad(sample, slope_one)
        bias_grad_one = lax.optimization_barrier(jnp.sum(slope_one.astype(jnp.float32), axis=(0, 2, 3, 4)))
        carry = (carry[0] + grad_one, carry[1] + bias_grad_one, carry[2] + grad_two, carry[3] + bias_grad_two)
        return (carry, feature[0])
    start = (jnp.zeros(kernel_one.shape, jnp.float32), jnp.zeros(bias_one.shape, jnp.float32), jnp.zeros(kernel_two.shape, jnp.float32), jnp.zeros(bias_two.shape, jnp.float32))
    totals, features = lax.scan(one_sample, start, (volume, cotangent))
    return (features, totals[0], totals[1], totals[2], totals[3])
```

```python
import functools

import jax
import jax.numpy as jnp
from jax import lax
from jax.experimental import pallas as pl
from jax.experimental.pallas import tpu as pltpu
from jax.sharding import PartitionSpec as P

F32 = jnp.float32
BF16 = jnp.bfloat16
MESH = pl.DeviceIdType.MESH
ROWS = 16
NT = (((1,), (1,)), ((), ()))


def kernel(n, nd, vol, w1, b1, w2, b2, cot, feat, g1_o, gb1_o, g2_o, gb2_o,
           vrecv, v32, stack_v, cot32, d_one, stack_a, res, slope3, sl, srecv,
           stack_s, feat32, slope31, sb, rb, red, gath,
           vs_sem, vr_sem, ss_sem, sr_sem, p1s, p1r, p2s, p2r):
    cin, planes, ny, nx = vol.shape
    cone, ctwo = w2.shape[1], w2.shape[2]
    cells = planes * ny * nx
    plane = ny * nx
    wide = planes + 2
    nsh = sb.shape[0]
    stride = n // nsh
    early = (27 * cone * ctwo // nx) // ROWS

    de = lax.axis_index("depth")
    me = lax.axis_index("dp") * nd + de
    dp = lax.axis_index("dp")

    def dev(t):
        return (lax.div(t, nd), lax.rem(t, nd))

    bar = pltpu.get_barrier_semaphore()

    @pl.loop(1, n)
    def _(d):
        pl.semaphore_signal(bar, inc=1, device_id=dev(lax.rem(me + d, n)), device_id_type=MESH)

    cot32[...] = cot[...].astype(F32).reshape(cot32.shape)
    wz = planes + 4
    zero8 = jnp.zeros((ny, nx), F32)
    for ch in range(8):
        for z in range(planes if ch < cin else wz):
            if ch < cin:
                v32[pl.ds((ch * wz + z + 2) * ny, ny), :] = vol[ch, z].astype(F32)
            else:
                v32[pl.ds((ch * wz + z) * ny, ny), :] = zero8
    lhs1 = []
    for ab in range(9):
        row = jnp.concatenate([w1[ab * 3 + c].astype(F32) for c in range(3)], axis=1)
        lhs1.append(jnp.concatenate([row, jnp.zeros((8 - cin, 3 * cone), F32)], axis=0))
    lhs1 = jnp.transpose(jnp.concatenate(lhs1, axis=0)).astype(BF16)
    lhs2 = jnp.concatenate(
        [jnp.concatenate([w2[ab * 3 + c].astype(F32) for c in range(3)], axis=1) for ab in range(9)], axis=0
    )
    lhs2 = jnp.transpose(lhs2).astype(BF16)
    lhs3 = jnp.concatenate(
        [
            jnp.concatenate([w2[(8 - ab) * 3 + 2 - c].astype(F32) for ab in range(9)], axis=1)
            for c in range(3)
        ],
        axis=0,
    ).astype(BF16)
    bias1 = jnp.transpose(jnp.broadcast_to(b1[...], (nx, cone)))
    bias2 = jnp.transpose(jnp.broadcast_to(b2[...], (nx, ctwo)))
    lane1 = lax.broadcasted_iota(jnp.int32, (cone, nx), 1)
    lane2 = lax.broadcasted_iota(jnp.int32, (ctwo, nx), 1)

    def right(t, lane):
        return jnp.where(lane == 0, 0.0, pltpu.roll(t, 1, 1))

    def left(t, lane):
        return jnp.where(lane == nx - 1, 0.0, pltpu.roll(t, nx - 1, 1))

    for z in range(planes):
        for a in range(3):
            for b, y in ((0, 0), (2, ny - 1)):
                lanes = pl.ds((z * ny + y) * nx, nx)
                stack_a[pl.ds((a * 3 + b) * cone, cone), lanes] = jnp.zeros((cone, nx), BF16)
                stack_s[pl.ds((a * 3 + b) * ctwo, ctwo), lanes] = jnp.zeros((ctwo, nx), BF16)
    stack_a[pl.ds(9 * cone, 16), :] = jnp.ones((16, cells), BF16)
    for z in range(wide):
        for a in range(3):
            for b, y in ((0, 0), (2, ny - 1)):
                stack_v[pl.ds((a * 3 + b) * 8, 8), pl.ds((z * ny + y) * nx, nx)] = zero8

    has_lo = de > 0
    has_hi = de < nd - 1
    pl.semaphore_wait(bar, n - 1)

    def vol_copy(up):
        src = vol.at[:, pl.ds(planes - 2, 2)] if up else vol.at[:, pl.ds(0, 2)]
        side = 0 if up else 1
        return pltpu.make_async_remote_copy(
            src_ref=src, dst_ref=vrecv.at[side], send_sem=vs_sem.at[side], recv_sem=vr_sem.at[side],
            device_id=(dp, de + 1 if up else de - 1), device_id_type=MESH)

    def slope_copy(up):
        src = sl.at[planes - 1] if up else sl.at[0]
        side = 0 if up else 1
        return pltpu.make_async_remote_copy(
            src_ref=src, dst_ref=srecv.at[side], send_sem=ss_sem.at[side], recv_sem=sr_sem.at[side],
            device_id=(dp, de + 1 if up else de - 1), device_id_type=MESH)

    @pl.when(has_hi)
    def _():
        vol_copy(True).start()

    @pl.when(has_lo)
    def _():
        vol_copy(False).start()

    for side, has, z0 in ((0, has_lo, 0), (1, has_hi, planes + 2)):
        @pl.when(has)
        def _(side=side, z0=z0):
            vol_copy(side == 0).wait_recv()
            for ch in range(cin):
                for z in range(2):
                    v32[pl.ds((ch * wz + z0 + z) * ny, ny), :] = vrecv[side, ch, z].astype(F32)

        @pl.when(jnp.logical_not(has))
        def _(z0=z0):
            for ch in range(cin):
                for z in range(2):
                    v32[pl.ds((ch * wz + z0 + z) * ny, ny), :] = zero8

    row8 = lax.broadcasted_iota(jnp.int32, (8, nx), 0)
    for zz in range(wz):
        for y in range(ny):
            tile = v32[pl.ds(zz * ny + y, 8, stride=wz * ny), :]
            for a in range(3):
                z = zz - a
                if not 0 <= z < wide:
                    continue
                for b in range(3):
                    yo = y + 1 - b
                    if not 0 <= yo < ny:
                        continue
                    t = jnp.where(row8 == cin, 1.0, tile) if (a == 1 and b == 1) else tile
                    stack_v[pl.ds((a * 3 + b) * 8, 8), pl.ds((z * ny + yo) * nx, nx)] = t

    for zz in range(wide):
        res[pl.ds(0, 3 * cone), pl.ds(0, plane)] = jnp.dot(
            lhs1, stack_v[:, pl.ds(zz * plane, plane)].astype(BF16), preferred_element_type=F32)
        for y in range(ny):
            lanes = pl.ds(y * nx, nx)
            pre = (right(res[pl.ds(0, cone), lanes], lane1) + res[pl.ds(cone, cone), lanes]
                   + left(res[pl.ds(2 * cone, cone), lanes], lane1) + bias1)
            s = 1.0 / (1.0 + jnp.exp(-pre))
            act = pre * s
            if 1 <= zz <= planes:
                d_one[:, pl.ds(((zz - 1) * ny + y) * nx, nx)] = s * (1.0 + pre * (1.0 - s))
            elif zz == 0:
                act = jnp.where(has_lo, act, 0.0)
            else:
                act = jnp.where(has_hi, act, 0.0)
            act = act.astype(BF16)
            for a in range(3):
                z = zz - a
                if not 0 <= z < planes:
                    continue
                for b in range(3):
                    yo = y + 1 - b
                    if 0 <= yo < ny:
                        stack_a[pl.ds((a * 3 + b) * cone, cone), pl.ds((z * ny + yo) * nx, nx)] = act

    for z in range(planes):
        res[...] = jnp.dot(lhs2, stack_a[pl.ds(0, 9 * cone), pl.ds(z * plane, plane)], preferred_element_type=F32)
        for y in range(ny):
            lanes = pl.ds(y * nx, nx)
            pre = (right(res[pl.ds(0, ctwo), lanes], lane2) + res[pl.ds(ctwo, ctwo), lanes]
                   + left(res[pl.ds(2 * ctwo, ctwo), lanes], lane2) + bias2)
            s = 1.0 / (1.0 + jnp.exp(-pre))
            feat32[pl.ds(z * ny + y, ctwo, stride=planes * ny), :] = pre * s
            up = cot32[pl.ds(z * ny + y, ctwo, stride=planes * ny), :]
            slope = (up * (s * (1.0 + pre * (1.0 - s)))).astype(BF16)
            sl[z, :, lanes] = slope
            slf = slope.astype(F32)
            cell = pl.ds((z * ny + y) * nx, nx)
            slope3[pl.ds(0, ctwo), cell] = left(slf, lane2).astype(BF16)
            slope3[pl.ds(ctwo, ctwo), cell] = slope
            slope3[pl.ds(2 * ctwo, ctwo), cell] = right(slf, lane2).astype(BF16)
            for a in range(3):
                zo = z + 1 - a
                if not 0 <= zo < planes:
                    continue
                for b in range(3):
                    yo = y + 1 - b
                    if 0 <= yo < ny:
                        stack_s[pl.ds((a * 3 + b) * ctwo, ctwo), pl.ds((zo * ny + yo) * nx, nx)] = slope

    @pl.when(has_hi)
    def _():
        slope_copy(True).start()

    @pl.when(has_lo)
    def _():
        slope_copy(False).start()

    g2 = lax.dot_general(stack_a[...], slope3[...], NT, preferred_element_type=F32)
    k2 = 9 * cone
    last = g2[0:k2, 2 * ctwo:3 * ctwo]
    sb[pl.ds(0, k2 // ROWS)] = g2[0:k2, 0:2 * ctwo].astype(BF16).reshape(k2 // ROWS, ROWS, nx)
    sb[pl.ds(k2 // ROWS, k2 // 2 // ROWS)] = jnp.concatenate(
        [last[0:k2 // 2], last[k2 // 2:k2]], axis=1).astype(BF16).reshape(k2 // 2 // ROWS, ROWS, nx)
    b2row = g2[k2:k2 + 8, 0:2 * ctwo]
    feat[...] = feat32[...].reshape(feat.shape).astype(BF16)

    def shard_copy(s):
        owner = s * stride
        slot = lax.rem(me - owner + n, n) - 1
        return pltpu.make_async_remote_copy(
            src_ref=sb.at[s], dst_ref=rb.at[slot], send_sem=p1s, recv_sem=p1r,
            device_id=dev(owner), device_id_type=MESH)

    mine = lax.div(me, stride)
    is_owner = lax.rem(me, stride) == 0

    @pl.loop(0, nsh)
    def _(d):
        s = lax.rem(mine + d, nsh)

        @pl.when((s < early) & (s * stride != me))
        def _():
            shard_copy(s).start()

    for side, has, a, z in ((0, has_lo, 0, 0), (1, has_hi, 2, planes - 1)):
        @pl.when(has)
        def _(side=side):
            slope_copy(side == 0).wait_recv()

        @pl.when(jnp.logical_not(has))
        def _(side=side):
            srecv[side] = jnp.zeros((ctwo, plane), BF16)

        for y in range(ny):
            tile = srecv[side, :, pl.ds(y * nx, nx)]
            for b in range(3):
                yo = y + 1 - b
                if 0 <= yo < ny:
                    stack_s[pl.ds((a * 3 + b) * ctwo, ctwo), pl.ds((z * ny + yo) * nx, nx)] = tile

    for z in range(planes):
        res[pl.ds(0, 3 * cone), :] = jnp.dot(
            lhs3, stack_s[:, pl.ds(z * plane, plane)], preferred_element_type=F32)
        for y in range(ny):
            lanes = pl.ds(y * nx, nx)
            cell = pl.ds((z * ny + y) * nx, nx)
            back = (right(res[pl.ds(0, cone), lanes], lane1) + res[pl.ds(cone, cone), lanes]
                    + left(res[pl.ds(2 * cone, cone), lanes], lane1))
            slope = (back * d_one[:, cell]).astype(BF16)
            slf = slope.astype(F32)
            slope31[pl.ds(0, cone), cell] = left(slf, lane1).astype(BF16)
            slope31[pl.ds(cone, cone), cell] = slope
            slope31[pl.ds(2 * cone, cone), cell] = right(slf, lane1).astype(BF16)

    g1 = lax.dot_general(stack_v[:, pl.ds(plane, cells)].astype(BF16), slope31[...], NT, preferred_element_type=F32)
    g1 = jnp.concatenate([g1, jnp.zeros((72, nx - 3 * cone), F32)], axis=1)
    sb[pl.ds(early, nsh - early)] = jnp.concatenate([g1, b2row], axis=0).astype(BF16).reshape(nsh - early, ROWS, nx)

    @pl.loop(early, nsh)
    def _(s):
        @pl.when(s * stride != me)
        def _():
            shard_copy(s).start()

    def out_copy(t):
        return pltpu.make_async_remote_copy(
            src_ref=red, dst_ref=gath.at[mine], send_sem=p2s, recv_sem=p2r,
            device_id=dev(t), device_id_type=MESH)

    def drain(buf, sem):
        pltpu.make_async_copy(buf, buf, sem).wait()

    @pl.when(is_owner)
    def _():
        drain(rb, p1r)
        total = sb[mine].astype(F32) + jnp.sum(rb[...].astype(F32), axis=0)
        red[...] = total.astype(BF16)
        gath[mine] = total.astype(BF16)

        @pl.loop(1, n)
        def _(d):
            out_copy(lax.rem(me + d, n)).start()

        drain(gath.at[pl.ds(0, nsh - 1)], p2r)
        drain(sb.at[pl.ds(0, nsh - 1)], p1s)

    if stride > 1:
        @pl.when(jnp.logical_not(is_owner))
        def _():
            drain(gath, p2r)
            drain(sb, p1s)

    full = gath[...].reshape(nsh * ROWS, nx).astype(F32)
    for ab in range(9):
        r = ab * cone
        g2_o[ab * 3] = full[r:r + cone, 0:ctwo]
        g2_o[ab * 3 + 1] = full[r:r + cone, ctwo:2 * ctwo]
    half = k2 // 2
    tail = jnp.concatenate([full[k2:k2 + half, 0:ctwo], full[k2:k2 + half, ctwo:2 * ctwo]], axis=0)
    for ab in range(9):
        g2_o[ab * 3 + 2] = tail[ab * cone:(ab + 1) * cone]
    base = early * ROWS
    for ab in range(9):
        for c in range(3):
            g1_o[ab * 3 + c] = full[base + ab * 8:base + ab * 8 + cin, c * cone:(c + 1) * cone]
    gb1_o[...] = full[base + 4 * 8 + cin:base + 4 * 8 + cin + 1, cone:2 * cone]
    gb2_o[...] = full[base + 72:base + 73, ctwo:2 * ctwo]

    @pl.when(has_hi)
    def _():
        vol_copy(True).wait_send()
        slope_copy(True).wait_send()

    @pl.when(has_lo)
    def _():
        vol_copy(False).wait_send()
        slope_copy(False).wait_send()

    @pl.when(is_owner)
    def _():
        @pl.loop(1, n)
        def _(d):
            out_copy(lax.rem(me + d, n)).wait_send()


def per_device(n, nd, volume, kernel_one, bias_one, kernel_two, bias_two, cotangent):
    _, cin, planes, ny, nx = volume.shape
    cone, ctwo = kernel_one.shape[0], kernel_two.shape[0]
    cells = planes * ny * nx
    nsh = (27 * cone * ctwo // nx + 80) // ROWS
    w1 = jnp.transpose(kernel_one, (2, 3, 4, 1, 0)).reshape(27, cin, cone)
    w2 = jnp.transpose(kernel_two, (2, 3, 4, 1, 0)).reshape(27, cone, ctwo)
    vm = pl.BlockSpec(memory_space=pltpu.VMEM)
    dma = pltpu.SemaphoreType.DMA
    outs = pl.pallas_call(
        functools.partial(kernel, n, nd),
        out_shape=(
            jax.ShapeDtypeStruct((ctwo, planes, ny, nx), BF16),
            jax.ShapeDtypeStruct((27, cin, cone), F32),
            jax.ShapeDtypeStruct((1, cone), F32),
            jax.ShapeDtypeStruct((27, cone, ctwo), F32),
            jax.ShapeDtypeStruct((1, ctwo), F32),
        ),
        in_specs=[vm] * 6,
        out_specs=[vm] * 5,
        scratch_shapes=[
            pltpu.VMEM((2, cin, 2, ny, nx), BF16),
            pltpu.VMEM((8 * (planes + 4) * ny, nx), F32),
            pltpu.VMEM((72, (planes + 2) * ny * nx), F32),
            pltpu.VMEM((ctwo * planes * ny, nx), F32),
            pltpu.VMEM((cone, cells), F32),
            pltpu.VMEM((9 * cone + 16, cells), BF16),
            pltpu.VMEM((3 * ctwo, ny * nx), F32),
            pltpu.VMEM((3 * ctwo, cells), BF16),
            pltpu.VMEM((planes, ctwo, ny * nx), BF16),
            pltpu.VMEM((2, ctwo, ny * nx), BF16),
            pltpu.VMEM((9 * ctwo, cells), BF16),
            pltpu.VMEM((ctwo * planes * ny, nx), F32),
            pltpu.VMEM((3 * cone, cells), BF16),
            pltpu.VMEM((nsh, ROWS, nx), BF16),
            pltpu.VMEM((n - 1, ROWS, nx), BF16),
            pltpu.VMEM((ROWS, nx), BF16),
            pltpu.VMEM((nsh, ROWS, nx), BF16),
            dma((2,)), dma((2,)), dma((2,)), dma((2,)),
            dma, dma, dma, dma,
        ],
        compiler_params=pltpu.CompilerParams(
            collective_id=0, has_side_effects=True, vmem_limit_bytes=48 * 1024 * 1024),
    )(
        volume.reshape(cin, planes, ny, nx), w1, bias_one.reshape(1, cone), w2,
        bias_two.reshape(1, ctwo), cotangent.reshape(ctwo, planes, ny, nx),
    )
    feat, g1, gb1, g2, gb2 = outs
    g1 = jnp.transpose(g1.reshape(3, 3, 3, cin, cone), (4, 3, 0, 1, 2))
    g2 = jnp.transpose(g2.reshape(3, 3, 3, cone, ctwo), (4, 3, 0, 1, 2))
    return feat[None], g1, gb1.reshape(cone), g2, gb2.reshape(ctwo)


def solution(mesh):
    nd = mesh.shape["depth"]
    n = mesh.shape["dp"] * nd
    return jax.shard_map(
        functools.partial(per_device, n, nd),
        mesh=mesh,
        in_specs=(
            P("dp", None, "depth", None, None),
            P(),
            P(),
            P(),
            P(),
            P("dp", None, "depth", None, None),
        ),
        out_specs=(P("dp", None, "depth", None, None), P(), P(), P(), P()),
        check_vma=False,
    )
```

```python
import functools

import jax
import jax.numpy as jnp
from jax import lax
from jax.experimental import pallas as pl
from jax.experimental.pallas import tpu as pltpu
from jax.sharding import PartitionSpec as P

F32 = jnp.float32
BF16 = jnp.bfloat16
MESH = pl.DeviceIdType.MESH
INNER = 4
NT = (((1,), (1,)), ((), ()))


def kernel(ni, nz, nd, vol_h, w1_h, b1_h, w2_h, b2_h, cot_h, feat, packed,
           vol, w1, b1, w2, b2, cot,
           vrecv, v32, stack_v, cot32, d_one, stack_a, res, slope3, sl, srecv,
           stack_s, feat32, slope31, sb, rb, zb, zsrc, gath,
           in_sem, vs_sem, vr_sem, ss_sem, sr_sem, p1s, p1r, pzs, pzr, p2s, p2r):
    cin, planes, ny, nx = vol.shape
    cone, ctwo = w2.shape[1], w2.shape[2]
    cells = planes * ny * nx
    plane = ny * nx
    wide = planes + 2
    nsh, rows = sb.shape[0], sb.shape[1]
    early = (27 * cone * ctwo // nx) // rows

    de = lax.axis_index("depth")
    dp = lax.axis_index("dp")
    zi = lax.div(dp, ni)
    me = lax.rem(dp, ni) * nd + de

    loads = [
        pltpu.make_async_copy(src, dst, in_sem.at[i])
        for i, (src, dst) in enumerate(
            ((vol_h, vol), (w1_h, w1), (b1_h, b1), (w2_h, w2), (b2_h, b2), (cot_h, cot)))
    ]
    for copy in loads:
        copy.start()

    def peer(j):
        return (zi * ni + lax.div(j, nd), lax.rem(j, nd))

    def column(k):
        return (k * ni + lax.rem(dp, ni), de)

    bar = pltpu.get_barrier_semaphore()

    @pl.loop(1, nsh)
    def _(d):
        pl.semaphore_signal(bar, inc=1, device_id=peer(lax.rem(me + d, nsh)), device_id_type=MESH)

    for d in range(1, nz):
        pl.semaphore_signal(bar, inc=1, device_id=column(lax.rem(zi + d, nz)), device_id_type=MESH)

    wz = planes + 4
    zero8 = jnp.zeros((ny, nx), F32)
    loads[0].wait()
    for ch in range(8):
        for z in range(planes if ch < cin else wz):
            if ch < cin:
                v32[pl.ds((ch * wz + z + 2) * ny, ny), :] = vol[ch, z].astype(F32)
            else:
                v32[pl.ds((ch * wz + z) * ny, ny), :] = zero8
    for copy in loads[1:5]:
        copy.wait()
    lhs1 = []
    for ab in range(9):
        row = jnp.concatenate([w1[ab * 3 + c].astype(F32) for c in range(3)], axis=1)
        lhs1.append(jnp.concatenate([row, jnp.zeros((8 - cin, 3 * cone), F32)], axis=0))
    lhs1 = jnp.transpose(jnp.concatenate(lhs1, axis=0)).astype(BF16)
    lhs2 = jnp.concatenate(
        [jnp.concatenate([w2[ab * 3 + c].astype(F32) for c in range(3)], axis=1) for ab in range(9)], axis=0
    )
    lhs2 = jnp.transpose(lhs2).astype(BF16)
    lhs3 = jnp.concatenate(
        [
            jnp.concatenate([w2[(8 - ab) * 3 + 2 - c].astype(F32) for ab in range(9)], axis=1)
            for c in range(3)
        ],
        axis=0,
    ).astype(BF16)
    bias1 = jnp.transpose(jnp.broadcast_to(b1[...], (nx, cone)))
    bias2 = jnp.transpose(jnp.broadcast_to(b2[...], (nx, ctwo)))
    lane1 = lax.broadcasted_iota(jnp.int32, (cone, nx), 1)
    lane2 = lax.broadcasted_iota(jnp.int32, (ctwo, nx), 1)

    def right(t, lane):
        return jnp.where(lane == 0, 0.0, pltpu.roll(t, 1, 1))

    def left(t, lane):
        return jnp.where(lane == nx - 1, 0.0, pltpu.roll(t, nx - 1, 1))

    for z in range(planes):
        for a in range(3):
            for b, y in ((0, 0), (2, ny - 1)):
                lanes = pl.ds((z * ny + y) * nx, nx)
                stack_a[pl.ds((a * 3 + b) * cone, cone), lanes] = jnp.zeros((cone, nx), BF16)
                stack_s[pl.ds((a * 3 + b) * ctwo, ctwo), lanes] = jnp.zeros((ctwo, nx), BF16)
    stack_a[pl.ds(9 * cone, 16), :] = jnp.ones((16, cells), BF16)
    for z in range(wide):
        for a in range(3):
            for b, y in ((0, 0), (2, ny - 1)):
                stack_v[pl.ds((a * 3 + b) * 8, 8), pl.ds((z * ny + y) * nx, nx)] = zero8

    loads[5].wait()
    cot32[...] = cot[...].astype(F32).reshape(cot32.shape)
    has_lo = de > 0
    has_hi = de < nd - 1
    pl.semaphore_wait(bar, nsh - 1 + nz - 1)

    def vol_copy(up):
        src = vol.at[:, pl.ds(planes - 2, 2)] if up else vol.at[:, pl.ds(0, 2)]
        side = 0 if up else 1
        return pltpu.make_async_remote_copy(
            src_ref=src, dst_ref=vrecv.at[side], send_sem=vs_sem.at[side], recv_sem=vr_sem.at[side],
            device_id=(dp, de + 1 if up else de - 1), device_id_type=MESH)

    def slope_copy(up):
        src = sl.at[planes - 1] if up else sl.at[0]
        side = 0 if up else 1
        return pltpu.make_async_remote_copy(
            src_ref=src, dst_ref=srecv.at[side], send_sem=ss_sem.at[side], recv_sem=sr_sem.at[side],
            device_id=(dp, de + 1 if up else de - 1), device_id_type=MESH)

    @pl.when(has_hi)
    def _():
        vol_copy(True).start()

    @pl.when(has_lo)
    def _():
        vol_copy(False).start()

    for side, has, z0 in ((0, has_lo, 0), (1, has_hi, planes + 2)):
        @pl.when(has)
        def _(side=side, z0=z0):
            vol_copy(side == 0).wait_recv()
            for ch in range(cin):
                for z in range(2):
                    v32[pl.ds((ch * wz + z0 + z) * ny, ny), :] = vrecv[side, ch, z].astype(F32)

        @pl.when(jnp.logical_not(has))
        def _(z0=z0):
            for ch in range(cin):
                for z in range(2):
                    v32[pl.ds((ch * wz + z0 + z) * ny, ny), :] = zero8

    row8 = lax.broadcasted_iota(jnp.int32, (8, nx), 0)
    for zz in range(wz):
        for y in range(ny):
            tile = v32[pl.ds(zz * ny + y, 8, stride=wz * ny), :]
            for a in range(3):
                z = zz - a
                if not 0 <= z < wide:
                    continue
                for b in range(3):
                    yo = y + 1 - b
                    if not 0 <= yo < ny:
                        continue
                    t = jnp.where(row8 == cin, 1.0, tile) if (a == 1 and b == 1) else tile
                    stack_v[pl.ds((a * 3 + b) * 8, 8), pl.ds((z * ny + yo) * nx, nx)] = t

    for zz in range(wide):
        res[pl.ds(0, 3 * cone), pl.ds(0, plane)] = jnp.dot(
            lhs1, stack_v[:, pl.ds(zz * plane, plane)].astype(BF16), preferred_element_type=F32)
        for y in range(ny):
            lanes = pl.ds(y * nx, nx)
            pre = (right(res[pl.ds(0, cone), lanes], lane1) + res[pl.ds(cone, cone), lanes]
                   + left(res[pl.ds(2 * cone, cone), lanes], lane1) + bias1)
            s = 1.0 / (1.0 + jnp.exp(-pre))
            act = pre * s
            if 1 <= zz <= planes:
                d_one[:, pl.ds(((zz - 1) * ny + y) * nx, nx)] = s * (1.0 + pre * (1.0 - s))
            elif zz == 0:
                act = jnp.where(has_lo, act, 0.0)
            else:
                act = jnp.where(has_hi, act, 0.0)
            act = act.astype(BF16)
            for a in range(3):
                z = zz - a
                if not 0 <= z < planes:
                    continue
                for b in range(3):
                    yo = y + 1 - b
                    if 0 <= yo < ny:
                        stack_a[pl.ds((a * 3 + b) * cone, cone), pl.ds((z * ny + yo) * nx, nx)] = act

    for z in range(planes):
        res[...] = jnp.dot(lhs2, stack_a[pl.ds(0, 9 * cone), pl.ds(z * plane, plane)], preferred_element_type=F32)
        for y in range(ny):
            lanes = pl.ds(y * nx, nx)
            pre = (right(res[pl.ds(0, ctwo), lanes], lane2) + res[pl.ds(ctwo, ctwo), lanes]
                   + left(res[pl.ds(2 * ctwo, ctwo), lanes], lane2) + bias2)
            s = 1.0 / (1.0 + jnp.exp(-pre))
            feat32[pl.ds(z * ny + y, ctwo, stride=planes * ny), :] = pre * s
            up = cot32[pl.ds(z * ny + y, ctwo, stride=planes * ny), :]
            slope = (up * (s * (1.0 + pre * (1.0 - s)))).astype(BF16)
            sl[z, :, lanes] = slope
            slf = slope.astype(F32)
            cell = pl.ds((z * ny + y) * nx, nx)
            slope3[pl.ds(0, ctwo), cell] = left(slf, lane2).astype(BF16)
            slope3[pl.ds(ctwo, ctwo), cell] = slope
            slope3[pl.ds(2 * ctwo, ctwo), cell] = right(slf, lane2).astype(BF16)
            for a in range(3):
                zo = z + 1 - a
                if not 0 <= zo < planes:
                    continue
                for b in range(3):
                    yo = y + 1 - b
                    if 0 <= yo < ny:
                        stack_s[pl.ds((a * 3 + b) * ctwo, ctwo), pl.ds((zo * ny + yo) * nx, nx)] = slope

    @pl.when(has_hi)
    def _():
        slope_copy(True).start()

    @pl.when(has_lo)
    def _():
        slope_copy(False).start()

    g2 = lax.dot_general(stack_a[...], slope3[...], NT, preferred_element_type=F32)
    k2 = 9 * cone
    last = g2[0:k2, 2 * ctwo:3 * ctwo]
    tail = jnp.concatenate([last[0:k2 // 2], last[k2 // 2:k2]], axis=1).astype(BF16)
    cut = early * rows - k2
    sb[pl.ds(0, early)] = jnp.concatenate(
        [g2[0:k2, 0:2 * ctwo].astype(BF16), tail[0:cut]], axis=0).reshape(early, rows, nx)
    b2row = g2[k2:k2 + 8, 0:2 * ctwo]

    def shard_copy(s):
        slot = lax.rem(me - s + nsh, nsh) - 1
        return pltpu.make_async_remote_copy(
            src_ref=sb.at[s], dst_ref=rb.at[slot], send_sem=p1s, recv_sem=p1r,
            device_id=peer(s), device_id_type=MESH)

    @pl.loop(1, nsh)
    def _(d):
        s = lax.rem(me + d, nsh)

        @pl.when(s < early)
        def _():
            shard_copy(s).start()

    for side, has, a, z in ((0, has_lo, 0, 0), (1, has_hi, 2, planes - 1)):
        @pl.when(has)
        def _(side=side):
            slope_copy(side == 0).wait_recv()

        @pl.when(jnp.logical_not(has))
        def _(side=side):
            srecv[side] = jnp.zeros((ctwo, plane), BF16)

        for y in range(ny):
            tile = srecv[side, :, pl.ds(y * nx, nx)]
            for b in range(3):
                yo = y + 1 - b
                if 0 <= yo < ny:
                    stack_s[pl.ds((a * 3 + b) * ctwo, ctwo), pl.ds((z * ny + yo) * nx, nx)] = tile

    for z in range(planes):
        res[pl.ds(0, 3 * cone), :] = jnp.dot(
            lhs3, stack_s[:, pl.ds(z * plane, plane)], preferred_element_type=F32)
        for y in range(ny):
            lanes = pl.ds(y * nx, nx)
            cell = pl.ds((z * ny + y) * nx, nx)
            back = (right(res[pl.ds(0, cone), lanes], lane1) + res[pl.ds(cone, cone), lanes]
                    + left(res[pl.ds(2 * cone, cone), lanes], lane1))
            slope = (back * d_one[:, cell]).astype(BF16)
            slf = slope.astype(F32)
            slope31[pl.ds(0, cone), cell] = left(slf, lane1).astype(BF16)
            slope31[pl.ds(cone, cone), cell] = slope
            slope31[pl.ds(2 * cone, cone), cell] = right(slf, lane1).astype(BF16)

    g1 = lax.dot_general(stack_v[:, pl.ds(plane, cells)].astype(BF16), slope31[...], NT, preferred_element_type=F32)
    g1 = jnp.concatenate([g1, jnp.zeros((72, nx - 3 * cone), F32)], axis=1)
    late = jnp.concatenate([g1, b2row], axis=0).astype(BF16)
    if cut < tail.shape[0]:
        late = jnp.concatenate([tail[cut:], late], axis=0)
    sb[pl.ds(early, nsh - early)] = late.reshape(nsh - early, rows, nx)

    @pl.loop(early, nsh)
    def _(s):
        @pl.when(s != me)
        def _():
            shard_copy(s).start()

    def drain(buf, sem):
        pltpu.make_async_copy(buf, buf, sem).wait()

    drain(rb, p1r)
    total = (sb[me].astype(F32) + jnp.sum(rb[...].astype(F32), axis=0)).astype(BF16)
    zsrc[...] = total
    zb[zi] = total

    def z_copy(d):
        return pltpu.make_async_remote_copy(
            src_ref=zsrc, dst_ref=zb.at[zi], send_sem=pzs, recv_sem=pzr,
            device_id=column(lax.rem(zi + d, nz)), device_id_type=MESH)

    for d in range(1, nz):
        z_copy(d).start()
    feat[...] = feat32[...].reshape(feat.shape).astype(BF16)
    drain(zb.at[pl.ds(0, nz - 1)], pzr)
    whole = zb[0].astype(F32)
    for k in range(1, nz):
        whole = whole + zb[k].astype(F32)
    gath[me] = whole.astype(BF16)

    def out_copy(d):
        return pltpu.make_async_remote_copy(
            src_ref=gath.at[me], dst_ref=gath.at[me], send_sem=p2s, recv_sem=p2r,
            device_id=peer(lax.rem(me + d, nsh)), device_id_type=MESH)

    @pl.loop(1, nsh)
    def _(d):
        out_copy(d).start()

    drain(gath.at[pl.ds(0, nsh - 1)], p2r)
    packed[...] = gath[...].reshape(packed.shape)

    drain(sb.at[pl.ds(0, nsh - 1)], p1s)
    drain(zb.at[pl.ds(0, nz - 1)], pzs)
    drain(gath.at[pl.ds(0, nsh - 1)], p2s)

    @pl.when(has_hi)
    def _():
        vol_copy(True).wait_send()
        slope_copy(True).wait_send()

    @pl.when(has_lo)
    def _():
        vol_copy(False).wait_send()
        slope_copy(False).wait_send()


def unpack(feat, packed, feat_o, g1_o, gb1_o, g2_o, gb2_o, g1, gb1, g2, gb2, sem):
    cin, cone, ctwo = g1.shape[1], g2.shape[1], g2.shape[2]
    k2 = 9 * cone
    half = k2 // 2
    base = k2 + half
    first = pltpu.make_async_copy(feat, feat_o, sem.at[0])
    first.start()
    full = packed[...].astype(F32)
    for ab in range(9):
        r = ab * cone
        g2[ab * 3] = full[r:r + cone, 0:ctwo]
        g2[ab * 3 + 1] = full[r:r + cone, ctwo:2 * ctwo]
    tail = jnp.concatenate([full[k2:base, 0:ctwo], full[k2:base, ctwo:2 * ctwo]], axis=0)
    for ab in range(9):
        g2[ab * 3 + 2] = tail[ab * cone:(ab + 1) * cone]
    copies = [first, pltpu.make_async_copy(g2, g2_o, sem.at[1])]
    copies[1].start()
    for ab in range(9):
        for c in range(3):
            g1[ab * 3 + c] = full[base + ab * 8:base + ab * 8 + cin, c * cone:(c + 1) * cone]
    gb1[...] = full[base + 4 * 8 + cin:base + 4 * 8 + cin + 1, cone:2 * cone]
    gb2[...] = full[base + 72:base + 73, ctwo:2 * ctwo]
    for i, (src, dst) in enumerate(((g1, g1_o), (gb1, gb1_o), (gb2, gb2_o))):
        copies.append(pltpu.make_async_copy(src, dst, sem.at[2 + i]))
        copies[-1].start()
    for copy in copies:
        copy.wait()


def per_device(ni, nz, nd, volume, kernel_one, bias_one, kernel_two, bias_two, cotangent):
    _, cin, planes, ny, nx = volume.shape
    cone, ctwo = kernel_one.shape[0], kernel_two.shape[0]
    cells = planes * ny * nx
    total = 27 * cone * ctwo // nx + 80
    nsh = ni * nd
    rows = total // nsh
    w1 = jnp.transpose(kernel_one, (2, 3, 4, 1, 0)).reshape(27, cin, cone)
    w2 = jnp.transpose(kernel_two, (2, 3, 4, 1, 0)).reshape(27, cone, ctwo)
    vm = pl.BlockSpec(memory_space=pltpu.VMEM)
    hbm = pl.BlockSpec(memory_space=pltpu.HBM)
    dma = pltpu.SemaphoreType.DMA
    feat, packed = pl.pallas_call(
        functools.partial(kernel, ni, nz, nd),
        out_shape=(
            jax.ShapeDtypeStruct((ctwo, planes, ny, nx), BF16),
            jax.ShapeDtypeStruct((total, nx), BF16),
        ),
        in_specs=[hbm] * 6,
        out_specs=[vm] * 2,
        scratch_shapes=[
            pltpu.VMEM((cin, planes, ny, nx), BF16),
            pltpu.VMEM((27, cin, cone), BF16),
            pltpu.VMEM((1, cone), F32),
            pltpu.VMEM((27, cone, ctwo), BF16),
            pltpu.VMEM((1, ctwo), F32),
            pltpu.VMEM((ctwo, planes, ny, nx), BF16),
            pltpu.VMEM((2, cin, 2, ny, nx), BF16),
            pltpu.VMEM((8 * (planes + 4) * ny, nx), F32),
            pltpu.VMEM((72, (planes + 2) * ny * nx), F32),
            pltpu.VMEM((ctwo * planes * ny, nx), F32),
            pltpu.VMEM((cone, cells), F32),
            pltpu.VMEM((9 * cone + 16, cells), BF16),
            pltpu.VMEM((3 * ctwo, ny * nx), F32),
            pltpu.VMEM((3 * ctwo, cells), BF16),
            pltpu.VMEM((planes, ctwo, ny * nx), BF16),
            pltpu.VMEM((2, ctwo, ny * nx), BF16),
            pltpu.VMEM((9 * ctwo, cells), BF16),
            pltpu.VMEM((ctwo * planes * ny, nx), F32),
            pltpu.VMEM((3 * cone, cells), BF16),
            pltpu.VMEM((nsh, rows, nx), BF16),
            pltpu.VMEM((nsh - 1, rows, nx), BF16),
            pltpu.VMEM((nz, rows, nx), BF16),
            pltpu.VMEM((rows, nx), BF16),
            pltpu.VMEM((nsh, rows, nx), BF16),
            dma((6,)),
            dma((2,)), dma((2,)), dma((2,)), dma((2,)),
            dma, dma, dma, dma, dma, dma,
        ],
        compiler_params=pltpu.CompilerParams(
            collective_id=0, has_side_effects=True, vmem_limit_bytes=48 * 1024 * 1024),
    )(*(
        pltpu.with_memory_space_constraint(x, pltpu.HBM)
        for x in (
            volume.reshape(cin, planes, ny, nx), w1, bias_one.reshape(1, cone), w2,
            bias_two.reshape(1, ctwo), cotangent.reshape(ctwo, planes, ny, nx))
    ))
    shapes = (((ctwo, planes, ny, nx), BF16), ((27, cin, cone), F32), ((1, cone), F32),
              ((27, cone, ctwo), F32), ((1, ctwo), F32))
    feat, g1, gb1, g2, gb2 = pl.pallas_call(
        unpack,
        out_shape=tuple(jax.ShapeDtypeStruct(*x) for x in shapes),
        in_specs=[vm] * 2,
        out_specs=[hbm] * 5,
        scratch_shapes=[pltpu.VMEM(*x) for x in shapes[1:]] + [dma((5,))],
        compiler_params=pltpu.CompilerParams(vmem_limit_bytes=8 * 1024 * 1024),
    )(feat, packed)
    g1 = jnp.transpose(g1.reshape(3, 3, 3, cin, cone), (4, 3, 0, 1, 2))
    g2 = jnp.transpose(g2.reshape(3, 3, 3, cone, ctwo), (4, 3, 0, 1, 2))
    return feat[None], g1, gb1.reshape(cone), g2, gb2.reshape(ctwo)


def solution(mesh):
    nd = mesh.shape["depth"]
    ni = min(INNER, mesh.shape["dp"])
    nz = mesh.shape["dp"] // ni
    return jax.shard_map(
        functools.partial(per_device, ni, nz, nd),
        mesh=mesh,
        in_specs=(
            P("dp", None, "depth", None, None),
            P(),
            P(),
            P(),
            P(),
            P("dp", None, "depth", None, None),
        ),
        out_specs=(P("dp", None, "depth", None, None), P(), P(), P(), P()),
        check_vma=False,
    )
```

```python
import functools

import jax
import jax.numpy as jnp
from jax import lax
from jax.experimental import pallas as pl
from jax.experimental.pallas import tpu as pltpu
from jax.sharding import PartitionSpec as P

F32 = jnp.float32
BF16 = jnp.bfloat16
MESH = pl.DeviceIdType.MESH
INNER = 4
NT = (((1,), (1,)), ((), ()))


def halo_parts(planes, nd):
    parts = ((1, 0, 3, 0),) if planes >= 3 else ((1, 1, 2, 0), (2, 0, 1, 2))
    return tuple(p for p in parts if p[0] < nd)


def kernel(ni, nz, nd, vol_h, w1_h, b1_h, w2_h, b2_h, cot_h, feat, packed,
           vol, w1, b1, w2, b2, cot,
           vrecv, v32, stack_v, cot32, d_one, stack_a, res, slope3, crecv, ccot32,
           stack_s, feat32, slope31, sb, rb, zb, zsrc, gath,
           in_sem, vs_sem, vr_sem, ss_sem, sr_sem, p1s, p1r, pzs, pzr, p2s, p2r):
    cin, planes, ny, nx = vol.shape
    cone, ctwo = w2.shape[1], w2.shape[2]
    cells = planes * ny * nx
    plane = ny * nx
    wide = planes + 4
    parts = halo_parts(planes, nd)
    nsh, rows = sb.shape[0], sb.shape[1]
    early = (27 * cone * ctwo // nx) // rows

    de = lax.axis_index("depth")
    dp = lax.axis_index("dp")
    zi = lax.div(dp, ni)
    me = lax.rem(dp, ni) * nd + de

    loads = [
        pltpu.make_async_copy(src, dst, in_sem.at[i])
        for i, (src, dst) in enumerate(
            ((vol_h, vol), (w1_h, w1), (b1_h, b1), (w2_h, w2), (b2_h, b2), (cot_h, cot)))
    ]
    for copy in loads:
        copy.start()

    def peer(j):
        return (zi * ni + lax.div(j, nd), lax.rem(j, nd))

    def column(k):
        return (k * ni + lax.rem(dp, ni), de)

    bar = pltpu.get_barrier_semaphore()

    @pl.loop(1, nsh)
    def _(d):
        pl.semaphore_signal(bar, inc=1, device_id=peer(lax.rem(me + d, nsh)), device_id_type=MESH)

    for d in range(1, nz):
        pl.semaphore_signal(bar, inc=1, device_id=column(lax.rem(zi + d, nz)), device_id_type=MESH)

    wz = planes + 6
    zero8 = jnp.zeros((ny, nx), F32)
    loads[0].wait()
    for ch in range(8):
        for z in range(planes if ch < cin else wz):
            if ch < cin:
                v32[pl.ds((ch * wz + z + 3) * ny, ny), :] = vol[ch, z].astype(F32)
            else:
                v32[pl.ds((ch * wz + z) * ny, ny), :] = zero8
    for copy in loads[1:5]:
        copy.wait()
    lhs1 = []
    for ab in range(9):
        row = jnp.concatenate([w1[ab * 3 + c].astype(F32) for c in range(3)], axis=1)
        lhs1.append(jnp.concatenate([row, jnp.zeros((8 - cin, 3 * cone), F32)], axis=0))
    lhs1 = jnp.transpose(jnp.concatenate(lhs1, axis=0)).astype(BF16)
    lhs2 = jnp.concatenate(
        [jnp.concatenate([w2[ab * 3 + c].astype(F32) for c in range(3)], axis=1) for ab in range(9)], axis=0
    )
    lhs2 = jnp.transpose(lhs2).astype(BF16)
    lhs3 = jnp.concatenate(
        [
            jnp.concatenate([w2[(8 - ab) * 3 + 2 - c].astype(F32) for ab in range(9)], axis=1)
            for c in range(3)
        ],
        axis=0,
    ).astype(BF16)
    bias1 = jnp.transpose(jnp.broadcast_to(b1[...], (nx, cone)))
    bias2 = jnp.transpose(jnp.broadcast_to(b2[...], (nx, ctwo)))
    lane1 = lax.broadcasted_iota(jnp.int32, (cone, nx), 1)
    lane2 = lax.broadcasted_iota(jnp.int32, (ctwo, nx), 1)

    def right(t, lane):
        return jnp.where(lane == 0, 0.0, pltpu.roll(t, 1, 1))

    def left(t, lane):
        return jnp.where(lane == nx - 1, 0.0, pltpu.roll(t, nx - 1, 1))

    for z in range(planes + 2):
        for a in range(3):
            for b, y in ((0, 0), (2, ny - 1)):
                lanes = pl.ds((z * ny + y) * nx, nx)
                stack_a[pl.ds((a * 3 + b) * cone, cone), lanes] = jnp.zeros((cone, nx), BF16)
                if z < planes:
                    stack_s[pl.ds((a * 3 + b) * ctwo, ctwo), lanes] = jnp.zeros((ctwo, nx), BF16)
    stack_a[pl.ds(9 * cone, 16), :] = jnp.ones((16, cells + 2 * plane), BF16)
    for z in range(wide):
        for a in range(3):
            for b, y in ((0, 0), (2, ny - 1)):
                stack_v[pl.ds((a * 3 + b) * 8, 8), pl.ds((z * ny + y) * nx, nx)] = zero8

    loads[5].wait()
    cot32[...] = cot[...].astype(F32).reshape(cot32.shape)
    has_lo = de > 0
    has_hi = de < nd - 1
    pl.semaphore_wait(bar, nsh - 1 + nz - 1)

    def vol_copy(side, i):
        dist, at, count, start = parts[i]
        src = planes - count if side == 0 else 0
        dst = at if side == 0 else start
        return pltpu.make_async_remote_copy(
            src_ref=vol.at[:, pl.ds(src, count)], dst_ref=vrecv.at[side, :, pl.ds(dst, count)],
            send_sem=vs_sem.at[side, i], recv_sem=vr_sem.at[side, i],
            device_id=(dp, de + dist if side == 0 else de - dist), device_id_type=MESH)

    def cot_copy(side):
        return pltpu.make_async_remote_copy(
            src_ref=cot.at[:, pl.ds(planes - 1 if side == 0 else 0, 1)], dst_ref=crecv.at[side],
            send_sem=ss_sem.at[side], recv_sem=sr_sem.at[side],
            device_id=(dp, de + 1 if side == 0 else de - 1), device_id_type=MESH)

    def sends(side, dist):
        return de < nd - dist if side == 0 else de >= dist

    def gets(side, dist):
        return de >= dist if side == 0 else de < nd - dist

    for i in range(len(parts)):
        for side in range(2):
            @pl.when(sends(side, parts[i][0]))
            def _(side=side, i=i):
                vol_copy(side, i).start()

    for side in range(2):
        @pl.when(sends(side, 1))
        def _(side=side):
            cot_copy(side).start()

    for side in range(2):
        z0 = 0 if side == 0 else planes + 3
        filled = set()
        for i, (dist, at, count, start) in enumerate(parts):
            first = at if side == 0 else start
            filled |= set(range(first, first + count))

            @pl.when(gets(side, dist))
            def _(side=side, i=i, first=first, count=count, z0=z0):
                vol_copy(side, i).wait_recv()
                for ch in range(cin):
                    for z in range(first, first + count):
                        v32[pl.ds((ch * wz + z0 + z) * ny, ny), :] = vrecv[side, ch, z].astype(F32)

            @pl.when(jnp.logical_not(gets(side, dist)))
            def _(first=first, count=count, z0=z0):
                for ch in range(cin):
                    for z in range(first, first + count):
                        v32[pl.ds((ch * wz + z0 + z) * ny, ny), :] = zero8

        for z in range(3):
            if z not in filled:
                for ch in range(cin):
                    v32[pl.ds((ch * wz + z0 + z) * ny, ny), :] = zero8

    row8 = lax.broadcasted_iota(jnp.int32, (8, nx), 0)
    for zz in range(wz):
        for y in range(ny):
            tile = v32[pl.ds(zz * ny + y, 8, stride=wz * ny), :]
            for a in range(3):
                z = zz - a
                if not 0 <= z < wide:
                    continue
                for b in range(3):
                    yo = y + 1 - b
                    if not 0 <= yo < ny:
                        continue
                    t = jnp.where(row8 == cin, 1.0, tile) if (a == 1 and b == 1) else tile
                    stack_v[pl.ds((a * 3 + b) * 8, 8), pl.ds((z * ny + yo) * nx, nx)] = t

    for zz in range(wide):
        res[pl.ds(0, 3 * cone), pl.ds(0, plane)] = jnp.dot(
            lhs1, stack_v[:, pl.ds(zz * plane, plane)].astype(BF16), preferred_element_type=F32)
        for y in range(ny):
            lanes = pl.ds(y * nx, nx)
            pre = (right(res[pl.ds(0, cone), lanes], lane1) + res[pl.ds(cone, cone), lanes]
                   + left(res[pl.ds(2 * cone, cone), lanes], lane1) + bias1)
            s = 1.0 / (1.0 + jnp.exp(-pre))
            act = pre * s
            if 2 <= zz < planes + 2:
                d_one[:, pl.ds(((zz - 2) * ny + y) * nx, nx)] = s * (1.0 + pre * (1.0 - s))
            elif zz < 2:
                act = jnp.where(has_lo, act, 0.0)
            else:
                act = jnp.where(has_hi, act, 0.0)
            act = act.astype(BF16)
            for a in range(3):
                z = zz - a
                if not 0 <= z < planes + 2:
                    continue
                for b in range(3):
                    yo = y + 1 - b
                    if 0 <= yo < ny:
                        stack_a[pl.ds((a * 3 + b) * cone, cone), pl.ds((z * ny + yo) * nx, nx)] = act

    def layer_two(z):
        res[...] = jnp.dot(
            lhs2, stack_a[pl.ds(0, 9 * cone), pl.ds((z + 1) * plane, plane)], preferred_element_type=F32)

    def pre_two(y):
        lanes = pl.ds(y * nx, nx)
        return (right(res[pl.ds(0, ctwo), lanes], lane2) + res[pl.ds(ctwo, ctwo), lanes]
                + left(res[pl.ds(2 * ctwo, ctwo), lanes], lane2) + bias2)

    for z in range(planes):
        layer_two(z)
        for y in range(ny):
            pre = pre_two(y)
            s = 1.0 / (1.0 + jnp.exp(-pre))
            feat32[pl.ds(z * ny + y, ctwo, stride=planes * ny), :] = pre * s
            up = cot32[pl.ds(z * ny + y, ctwo, stride=planes * ny), :]
            slope = (up * (s * (1.0 + pre * (1.0 - s)))).astype(BF16)
            slf = slope.astype(F32)
            cell = pl.ds((z * ny + y) * nx, nx)
            slope3[pl.ds(0, ctwo), cell] = left(slf, lane2).astype(BF16)
            slope3[pl.ds(ctwo, ctwo), cell] = slope
            slope3[pl.ds(2 * ctwo, ctwo), cell] = right(slf, lane2).astype(BF16)
            for a in range(3):
                zo = z + 1 - a
                if not 0 <= zo < planes:
                    continue
                for b in range(3):
                    yo = y + 1 - b
                    if 0 <= yo < ny:
                        stack_s[pl.ds((a * 3 + b) * ctwo, ctwo), pl.ds((zo * ny + yo) * nx, nx)] = slope

    g2 = lax.dot_general(stack_a[:, pl.ds(plane, cells)], slope3[...], NT, preferred_element_type=F32)
    k2 = 9 * cone
    last = g2[0:k2, 2 * ctwo:3 * ctwo]
    tail = jnp.concatenate([last[0:k2 // 2], last[k2 // 2:k2]], axis=1).astype(BF16)
    cut = early * rows - k2
    sb[pl.ds(0, early)] = jnp.concatenate(
        [g2[0:k2, 0:2 * ctwo].astype(BF16), tail[0:cut]], axis=0).reshape(early, rows, nx)
    b2row = g2[k2:k2 + 8, 0:2 * ctwo]

    def shard_copy(s):
        slot = lax.rem(me - s + nsh, nsh) - 1
        return pltpu.make_async_remote_copy(
            src_ref=sb.at[s], dst_ref=rb.at[slot], send_sem=p1s, recv_sem=p1r,
            device_id=peer(s), device_id_type=MESH)

    @pl.loop(1, nsh)
    def _(d):
        s = lax.rem(me + d, nsh)

        @pl.when(s < early)
        def _():
            shard_copy(s).start()

    for side, a, z in ((0, 0, 0), (1, 2, planes - 1)):
        def place(y, tile, a=a, z=z):
            for b in range(3):
                yo = y + 1 - b
                if 0 <= yo < ny:
                    stack_s[pl.ds((a * 3 + b) * ctwo, ctwo), pl.ds((z * ny + yo) * nx, nx)] = tile

        @pl.when(gets(side, 1))
        def _(side=side, place=place):
            layer_two(-1 if side == 0 else planes)
            cot_copy(side).wait_recv()
            ccot32[...] = crecv[side].astype(F32).reshape(ccot32.shape)
            for y in range(ny):
                pre = pre_two(y)
                s = 1.0 / (1.0 + jnp.exp(-pre))
                up = ccot32[pl.ds(y, ctwo, stride=ny), :]
                place(y, (up * (s * (1.0 + pre * (1.0 - s)))).astype(BF16))

        @pl.when(jnp.logical_not(gets(side, 1)))
        def _(place=place):
            for y in range(ny):
                place(y, jnp.zeros((ctwo, nx), BF16))

    for z in range(planes):
        res[pl.ds(0, 3 * cone), :] = jnp.dot(
            lhs3, stack_s[:, pl.ds(z * plane, plane)], preferred_element_type=F32)
        for y in range(ny):
            lanes = pl.ds(y * nx, nx)
            cell = pl.ds((z * ny + y) * nx, nx)
            back = (right(res[pl.ds(0, cone), lanes], lane1) + res[pl.ds(cone, cone), lanes]
                    + left(res[pl.ds(2 * cone, cone), lanes], lane1))
            slope = (back * d_one[:, cell]).astype(BF16)
            slf = slope.astype(F32)
            slope31[pl.ds(0, cone), cell] = left(slf, lane1).astype(BF16)
            slope31[pl.ds(cone, cone), cell] = slope
            slope31[pl.ds(2 * cone, cone), cell] = right(slf, lane1).astype(BF16)

    g1 = lax.dot_general(stack_v[:, pl.ds(2 * plane, cells)].astype(BF16), slope31[...], NT, preferred_element_type=F32)
    g1 = jnp.concatenate([g1, jnp.zeros((72, nx - 3 * cone), F32)], axis=1)
    late = jnp.concatenate([g1, b2row], axis=0).astype(BF16)
    if cut < tail.shape[0]:
        late = jnp.concatenate([tail[cut:], late], axis=0)
    sb[pl.ds(early, nsh - early)] = late.reshape(nsh - early, rows, nx)

    @pl.loop(early, nsh)
    def _(s):
        @pl.when(s != me)
        def _():
            shard_copy(s).start()

    def drain(buf, sem):
        pltpu.make_async_copy(buf, buf, sem).wait()

    drain(rb, p1r)
    total = (sb[me].astype(F32) + jnp.sum(rb[...].astype(F32), axis=0)).astype(BF16)
    zsrc[...] = total
    zb[zi] = total

    def z_copy(d):
        return pltpu.make_async_remote_copy(
            src_ref=zsrc, dst_ref=zb.at[zi], send_sem=pzs, recv_sem=pzr,
            device_id=column(lax.rem(zi + d, nz)), device_id_type=MESH)

    for d in range(1, nz):
        z_copy(d).start()
    feat[...] = feat32[...].reshape(feat.shape).astype(BF16)
    drain(zb.at[pl.ds(0, nz - 1)], pzr)
    whole = zb[0].astype(F32)
    for k in range(1, nz):
        whole = whole + zb[k].astype(F32)
    gath[me] = whole.astype(BF16)

    def out_copy(d):
        return pltpu.make_async_remote_copy(
            src_ref=gath.at[me], dst_ref=gath.at[me], send_sem=p2s, recv_sem=p2r,
            device_id=peer(lax.rem(me + d, nsh)), device_id_type=MESH)

    @pl.loop(1, nsh)
    def _(d):
        out_copy(d).start()

    drain(gath.at[pl.ds(0, nsh - 1)], p2r)
    packed[...] = gath[...].reshape(packed.shape)

    drain(sb.at[pl.ds(0, nsh - 1)], p1s)
    drain(zb.at[pl.ds(0, nz - 1)], pzs)
    drain(gath.at[pl.ds(0, nsh - 1)], p2s)

    for side in range(2):
        for i in range(len(parts)):
            @pl.when(sends(side, parts[i][0]))
            def _(side=side, i=i):
                vol_copy(side, i).wait_send()

        @pl.when(sends(side, 1))
        def _(side=side):
            cot_copy(side).wait_send()


def unpack(feat, packed, feat_o, g1_o, gb1_o, g2_o, gb2_o, g1, gb1, g2, gb2, sem):
    cin, cone, ctwo = g1.shape[1], g2.shape[1], g2.shape[2]
    k2 = 9 * cone
    half = k2 // 2
    base = k2 + half
    first = pltpu.make_async_copy(feat, feat_o, sem.at[0])
    first.start()
    full = packed[...].astype(F32)
    for ab in range(9):
        r = ab * cone
        g2[ab * 3] = full[r:r + cone, 0:ctwo]
        g2[ab * 3 + 1] = full[r:r + cone, ctwo:2 * ctwo]
    tail = jnp.concatenate([full[k2:base, 0:ctwo], full[k2:base, ctwo:2 * ctwo]], axis=0)
    for ab in range(9):
        g2[ab * 3 + 2] = tail[ab * cone:(ab + 1) * cone]
    copies = [first, pltpu.make_async_copy(g2, g2_o, sem.at[1])]
    copies[1].start()
    for ab in range(9):
        for c in range(3):
            g1[ab * 3 + c] = full[base + ab * 8:base + ab * 8 + cin, c * cone:(c + 1) * cone]
    gb1[...] = full[base + 4 * 8 + cin:base + 4 * 8 + cin + 1, cone:2 * cone]
    gb2[...] = full[base + 72:base + 73, ctwo:2 * ctwo]
    for i, (src, dst) in enumerate(((g1, g1_o), (gb1, gb1_o), (gb2, gb2_o))):
        copies.append(pltpu.make_async_copy(src, dst, sem.at[2 + i]))
        copies[-1].start()
    for copy in copies:
        copy.wait()


def per_device(ni, nz, nd, volume, kernel_one, bias_one, kernel_two, bias_two, cotangent):
    _, cin, planes, ny, nx = volume.shape
    cone, ctwo = kernel_one.shape[0], kernel_two.shape[0]
    cells = planes * ny * nx
    total = 27 * cone * ctwo // nx + 80
    nsh = ni * nd
    rows = total // nsh
    w1 = jnp.transpose(kernel_one, (2, 3, 4, 1, 0)).reshape(27, cin, cone)
    w2 = jnp.transpose(kernel_two, (2, 3, 4, 1, 0)).reshape(27, cone, ctwo)
    vm = pl.BlockSpec(memory_space=pltpu.VMEM)
    hbm = pl.BlockSpec(memory_space=pltpu.HBM)
    dma = pltpu.SemaphoreType.DMA
    feat, packed = pl.pallas_call(
        functools.partial(kernel, ni, nz, nd),
        out_shape=(
            jax.ShapeDtypeStruct((ctwo, planes, ny, nx), BF16),
            jax.ShapeDtypeStruct((total, nx), BF16),
        ),
        in_specs=[hbm] * 6,
        out_specs=[vm] * 2,
        scratch_shapes=[
            pltpu.VMEM((cin, planes, ny, nx), BF16),
            pltpu.VMEM((27, cin, cone), BF16),
            pltpu.VMEM((1, cone), F32),
            pltpu.VMEM((27, cone, ctwo), BF16),
            pltpu.VMEM((1, ctwo), F32),
            pltpu.VMEM((ctwo, planes, ny, nx), BF16),
            pltpu.VMEM((2, cin, 3, ny, nx), BF16),
            pltpu.VMEM((8 * (planes + 6) * ny, nx), F32),
            pltpu.VMEM((72, (planes + 4) * ny * nx), F32),
            pltpu.VMEM((ctwo * planes * ny, nx), F32),
            pltpu.VMEM((cone, cells), F32),
            pltpu.VMEM((9 * cone + 16, cells + 2 * ny * nx), BF16),
            pltpu.VMEM((3 * ctwo, ny * nx), F32),
            pltpu.VMEM((3 * ctwo, cells), BF16),
            pltpu.VMEM((2, ctwo, 1, ny, nx), BF16),
            pltpu.VMEM((ctwo * ny, nx), F32),
            pltpu.VMEM((9 * ctwo, cells), BF16),
            pltpu.VMEM((ctwo * planes * ny, nx), F32),
            pltpu.VMEM((3 * cone, cells), BF16),
            pltpu.VMEM((nsh, rows, nx), BF16),
            pltpu.VMEM((nsh - 1, rows, nx), BF16),
            pltpu.VMEM((nz, rows, nx), BF16),
            pltpu.VMEM((rows, nx), BF16),
            pltpu.VMEM((nsh, rows, nx), BF16),
            dma((6,)),
            dma((2, max(1, len(halo_parts(planes, nd))))), dma((2, max(1, len(halo_parts(planes, nd))))), dma((2,)), dma((2,)),
            dma, dma, dma, dma, dma, dma,
        ],
        compiler_params=pltpu.CompilerParams(
            collective_id=0, has_side_effects=True, vmem_limit_bytes=48 * 1024 * 1024),
    )(*(
        pltpu.with_memory_space_constraint(x, pltpu.HBM)
        for x in (
            volume.reshape(cin, planes, ny, nx), w1, bias_one.reshape(1, cone), w2,
            bias_two.reshape(1, ctwo), cotangent.reshape(ctwo, planes, ny, nx))
    ))
    shapes = (((ctwo, planes, ny, nx), BF16), ((27, cin, cone), F32), ((1, cone), F32),
              ((27, cone, ctwo), F32), ((1, ctwo), F32))
    feat, g1, gb1, g2, gb2 = pl.pallas_call(
        unpack,
        out_shape=tuple(jax.ShapeDtypeStruct(*x) for x in shapes),
        in_specs=[vm] * 2,
        out_specs=[hbm] * 5,
        scratch_shapes=[pltpu.VMEM(*x) for x in shapes[1:]] + [dma((5,))],
        compiler_params=pltpu.CompilerParams(vmem_limit_bytes=8 * 1024 * 1024),
    )(feat, packed)
    g1 = jnp.transpose(g1.reshape(3, 3, 3, cin, cone), (4, 3, 0, 1, 2))
    g2 = jnp.transpose(g2.reshape(3, 3, 3, cone, ctwo), (4, 3, 0, 1, 2))
    return feat[None], g1, gb1.reshape(cone), g2, gb2.reshape(ctwo)


def solution(mesh):
    nd = mesh.shape["depth"]
    ni = min(INNER, mesh.shape["dp"])
    nz = mesh.shape["dp"] // ni
    return jax.shard_map(
        functools.partial(per_device, ni, nz, nd),
        mesh=mesh,
        in_specs=(
            P("dp", None, "depth", None, None),
            P(),
            P(),
            P(),
            P(),
            P("dp", None, "depth", None, None),
        ),
        out_specs=(P("dp", None, "depth", None, None), P(), P(), P(), P()),
        check_vma=False,
    )
```

```python
import functools

import jax
import jax.numpy as jnp
from jax import lax
from jax.experimental import pallas as pl
from jax.experimental.pallas import tpu as pltpu
from jax.sharding import PartitionSpec as P

F32 = jnp.float32
BF16 = jnp.bfloat16
MESH = pl.DeviceIdType.MESH
INNER = 4
NT = (((1,), (1,)), ((), ()))


def halo_parts(planes, nd):
    parts = ((1, 0, 3, 0),) if planes >= 3 else ((1, 1, 2, 0), (2, 0, 1, 2))
    return tuple(p for p in parts if p[0] < nd)


def kernel(ni, nz, nd, vol_h, w1_h, b1_h, w2_h, b2_h, cot_h, feat, packed,
           vol, w1, b1, w2, b2, cot,
           vrecv, v32, stack_v, cot32, d_one, stack_a, res, slope3, crecv, ccot32,
           stack_s, feat32, slope31, sb, rb, zb, zsrc, gath,
           in_sem, vs_sem, vr_sem, ss_sem, sr_sem, p1s, p1r, pzs, pzr, p2s, p2r):
    cin, planes, ny, nx = vol.shape
    cone, ctwo = w2.shape[1], w2.shape[2]
    cells = planes * ny * nx
    plane = ny * nx
    wide = planes + 4
    parts = halo_parts(planes, nd)
    halves, rows = zb.shape[0], sb.shape[1]
    nsh = sb.shape[0] // halves
    early = (27 * cone * ctwo // nx) // rows

    de = lax.axis_index("depth")
    dp = lax.axis_index("dp")
    zi = lax.div(dp, ni)
    me = lax.rem(dp, ni) * nd + de

    def peer(j):
        return (zi * ni + lax.div(j, nd), lax.rem(j, nd))

    def column(k):
        return (k * ni + lax.rem(dp, ni), de)

    bar = pltpu.get_barrier_semaphore()

    for d in range(1, nz):
        pl.semaphore_signal(bar, inc=1, device_id=column(lax.rem(zi + d, nz)), device_id_type=MESH)

    @pl.loop(1, nsh)
    def _(d):
        pl.semaphore_signal(bar, inc=1, device_id=peer(lax.rem(me + d, nsh)), device_id_type=MESH)

    loads = [
        pltpu.make_async_copy(src, dst, in_sem.at[i])
        for i, (src, dst) in enumerate(
            ((vol_h, vol), (w1_h, w1), (b1_h, b1), (w2_h, w2), (b2_h, b2), (cot_h, cot)))
    ]
    for copy in loads:
        copy.start()

    wz = planes + 6
    zero8 = jnp.zeros((ny, nx), F32)
    loads[0].wait()
    for ch in range(8):
        for z in range(planes if ch < cin else wz):
            if ch < cin:
                v32[pl.ds((ch * wz + z + 3) * ny, ny), :] = vol[ch, z].astype(F32)
            else:
                v32[pl.ds((ch * wz + z) * ny, ny), :] = zero8
    for copy in loads[1:5]:
        copy.wait()
    lhs1 = []
    for ab in range(9):
        row = jnp.concatenate([w1[ab * 3 + c].astype(F32) for c in range(3)], axis=1)
        lhs1.append(jnp.concatenate([row, jnp.zeros((8 - cin, 3 * cone), F32)], axis=0))
    lhs1 = jnp.transpose(jnp.concatenate(lhs1, axis=0)).astype(BF16)
    lhs2 = jnp.concatenate(
        [jnp.concatenate([w2[ab * 3 + c].astype(F32) for c in range(3)], axis=1) for ab in range(9)], axis=0
    )
    lhs2 = jnp.transpose(lhs2).astype(BF16)
    lhs3 = jnp.concatenate(
        [
            jnp.concatenate([w2[(8 - ab) * 3 + 2 - c].astype(F32) for ab in range(9)], axis=1)
            for c in range(3)
        ],
        axis=0,
    ).astype(BF16)
    bias1 = jnp.transpose(jnp.broadcast_to(b1[...], (nx, cone)))
    bias2 = jnp.transpose(jnp.broadcast_to(b2[...], (nx, ctwo)))
    lane1 = lax.broadcasted_iota(jnp.int32, (cone, nx), 1)
    lane2 = lax.broadcasted_iota(jnp.int32, (ctwo, nx), 1)

    def right(t, lane):
        return jnp.where(lane == 0, 0.0, pltpu.roll(t, 1, 1))

    def left(t, lane):
        return jnp.where(lane == nx - 1, 0.0, pltpu.roll(t, nx - 1, 1))

    for z in range(planes + 2):
        for a in range(3):
            for b, y in ((0, 0), (2, ny - 1)):
                lanes = pl.ds((z * ny + y) * nx, nx)
                stack_a[pl.ds((a * 3 + b) * cone, cone), lanes] = jnp.zeros((cone, nx), BF16)
                if z < planes:
                    stack_s[pl.ds((a * 3 + b) * ctwo, ctwo), lanes] = jnp.zeros((ctwo, nx), BF16)
    stack_a[pl.ds(9 * cone, 16), :] = jnp.ones((16, cells + 2 * plane), BF16)
    for z in range(wide):
        for a in range(3):
            for b, y in ((0, 0), (2, ny - 1)):
                stack_v[pl.ds((a * 3 + b) * 8, 8), pl.ds((z * ny + y) * nx, nx)] = zero8

    loads[5].wait()
    cot32[...] = cot[...].astype(F32).reshape(cot32.shape)
    has_lo = de > 0
    has_hi = de < nd - 1
    pl.semaphore_wait(bar, nsh - 1 + nz - 1)

    def vol_copy(side, i):
        dist, at, count, start = parts[i]
        src = planes - count if side == 0 else 0
        dst = at if side == 0 else start
        return pltpu.make_async_remote_copy(
            src_ref=vol.at[:, pl.ds(src, count)], dst_ref=vrecv.at[side, :, pl.ds(dst, count)],
            send_sem=vs_sem.at[side, i], recv_sem=vr_sem.at[side, i],
            device_id=(dp, de + dist if side == 0 else de - dist), device_id_type=MESH)

    def cot_copy(side):
        return pltpu.make_async_remote_copy(
            src_ref=cot.at[:, pl.ds(planes - 1 if side == 0 else 0, 1)], dst_ref=crecv.at[side],
            send_sem=ss_sem.at[side], recv_sem=sr_sem.at[side],
            device_id=(dp, de + 1 if side == 0 else de - 1), device_id_type=MESH)

    def sends(side, dist):
        return de < nd - dist if side == 0 else de >= dist

    def gets(side, dist):
        return de >= dist if side == 0 else de < nd - dist

    for i in range(len(parts)):
        for side in range(2):
            @pl.when(sends(side, parts[i][0]))
            def _(side=side, i=i):
                vol_copy(side, i).start()

    for side in range(2):
        @pl.when(sends(side, 1))
        def _(side=side):
            cot_copy(side).start()

    for side in range(2):
        z0 = 0 if side == 0 else planes + 3
        filled = set()
        for i, (dist, at, count, start) in enumerate(parts):
            first = at if side == 0 else start
            filled |= set(range(first, first + count))

            @pl.when(gets(side, dist))
            def _(side=side, i=i, first=first, count=count, z0=z0):
                vol_copy(side, i).wait_recv()
                for ch in range(cin):
                    for z in range(first, first + count):
                        v32[pl.ds((ch * wz + z0 + z) * ny, ny), :] = vrecv[side, ch, z].astype(F32)

            @pl.when(jnp.logical_not(gets(side, dist)))
            def _(first=first, count=count, z0=z0):
                for ch in range(cin):
                    for z in range(first, first + count):
                        v32[pl.ds((ch * wz + z0 + z) * ny, ny), :] = zero8

        for z in range(3):
            if z not in filled:
                for ch in range(cin):
                    v32[pl.ds((ch * wz + z0 + z) * ny, ny), :] = zero8

    row8 = lax.broadcasted_iota(jnp.int32, (8, nx), 0)
    for zz in range(wz):
        for y in range(ny):
            tile = v32[pl.ds(zz * ny + y, 8, stride=wz * ny), :]
            for a in range(3):
                z = zz - a
                if not 0 <= z < wide:
                    continue
                for b in range(3):
                    yo = y + 1 - b
                    if not 0 <= yo < ny:
                        continue
                    t = jnp.where(row8 == cin, 1.0, tile) if (a == 1 and b == 1) else tile
                    stack_v[pl.ds((a * 3 + b) * 8, 8), pl.ds((z * ny + yo) * nx, nx)] = t

    for zz in range(wide):
        res[pl.ds(0, 3 * cone), pl.ds(0, plane)] = jnp.dot(
            lhs1, stack_v[:, pl.ds(zz * plane, plane)].astype(BF16), preferred_element_type=F32)
        for y in range(ny):
            lanes = pl.ds(y * nx, nx)
            pre = (right(res[pl.ds(0, cone), lanes], lane1) + res[pl.ds(cone, cone), lanes]
                   + left(res[pl.ds(2 * cone, cone), lanes], lane1) + bias1)
            s = 1.0 / (1.0 + jnp.exp(-pre))
            act = pre * s
            if 2 <= zz < planes + 2:
                d_one[:, pl.ds(((zz - 2) * ny + y) * nx, nx)] = s * (1.0 + pre * (1.0 - s))
            elif zz < 2:
                act = jnp.where(has_lo, act, 0.0)
            else:
                act = jnp.where(has_hi, act, 0.0)
            act = act.astype(BF16)
            for a in range(3):
                z = zz - a
                if not 0 <= z < planes + 2:
                    continue
                for b in range(3):
                    yo = y + 1 - b
                    if 0 <= yo < ny:
                        stack_a[pl.ds((a * 3 + b) * cone, cone), pl.ds((z * ny + yo) * nx, nx)] = act

    def layer_two(z):
        res[...] = jnp.dot(
            lhs2, stack_a[pl.ds(0, 9 * cone), pl.ds((z + 1) * plane, plane)], preferred_element_type=F32)

    def pre_two(y):
        lanes = pl.ds(y * nx, nx)
        return (right(res[pl.ds(0, ctwo), lanes], lane2) + res[pl.ds(ctwo, ctwo), lanes]
                + left(res[pl.ds(2 * ctwo, ctwo), lanes], lane2) + bias2)

    for z in range(planes):
        layer_two(z)
        for y in range(ny):
            pre = pre_two(y)
            s = 1.0 / (1.0 + jnp.exp(-pre))
            feat32[pl.ds(z * ny + y, ctwo, stride=planes * ny), :] = pre * s
            up = cot32[pl.ds(z * ny + y, ctwo, stride=planes * ny), :]
            slope = (up * (s * (1.0 + pre * (1.0 - s)))).astype(BF16)
            slf = slope.astype(F32)
            cell = pl.ds((z * ny + y) * nx, nx)
            slope3[pl.ds(0, ctwo), cell] = left(slf, lane2).astype(BF16)
            slope3[pl.ds(ctwo, ctwo), cell] = slope
            slope3[pl.ds(2 * ctwo, ctwo), cell] = right(slf, lane2).astype(BF16)
            for a in range(3):
                zo = z + 1 - a
                if not 0 <= zo < planes:
                    continue
                for b in range(3):
                    yo = y + 1 - b
                    if 0 <= yo < ny:
                        stack_s[pl.ds((a * 3 + b) * ctwo, ctwo), pl.ds((zo * ny + yo) * nx, nx)] = slope

    g2 = lax.dot_general(stack_a[:, pl.ds(plane, cells)], slope3[...], NT, preferred_element_type=F32)
    k2 = 9 * cone
    last = g2[0:k2, 2 * ctwo:3 * ctwo]
    tail = jnp.concatenate([last[0:k2 // 2], last[k2 // 2:k2]], axis=1).astype(BF16)
    cut = early * rows - k2
    sb[pl.ds(0, early)] = jnp.concatenate(
        [g2[0:k2, 0:2 * ctwo].astype(BF16), tail[0:cut]], axis=0).reshape(early, rows, nx)
    b2row = g2[k2:k2 + 8, 0:2 * ctwo]

    def shard_copy(h, s):
        slot = lax.rem(me - s + nsh, nsh) - 1
        return pltpu.make_async_remote_copy(
            src_ref=sb.at[h * nsh + s], dst_ref=rb.at[h, slot], send_sem=p1s, recv_sem=p1r.at[h],
            device_id=peer(s), device_id_type=MESH)

    for h in range(halves):
        @pl.loop(1, nsh)
        def _(d, h=h):
            s = lax.rem(me + d, nsh)

            @pl.when(h * nsh + s < early)
            def _():
                shard_copy(h, s).start()

    for side, a, z in ((0, 0, 0), (1, 2, planes - 1)):
        def place(y, tile, a=a, z=z):
            for b in range(3):
                yo = y + 1 - b
                if 0 <= yo < ny:
                    stack_s[pl.ds((a * 3 + b) * ctwo, ctwo), pl.ds((z * ny + yo) * nx, nx)] = tile

        @pl.when(gets(side, 1))
        def _(side=side, place=place):
            layer_two(-1 if side == 0 else planes)
            cot_copy(side).wait_recv()
            ccot32[...] = crecv[side].astype(F32).reshape(ccot32.shape)
            for y in range(ny):
                pre = pre_two(y)
                s = 1.0 / (1.0 + jnp.exp(-pre))
                up = ccot32[pl.ds(y, ctwo, stride=ny), :]
                place(y, (up * (s * (1.0 + pre * (1.0 - s)))).astype(BF16))

        @pl.when(jnp.logical_not(gets(side, 1)))
        def _(place=place):
            for y in range(ny):
                place(y, jnp.zeros((ctwo, nx), BF16))

    for z in range(planes):
        res[pl.ds(0, 3 * cone), :] = jnp.dot(
            lhs3, stack_s[:, pl.ds(z * plane, plane)], preferred_element_type=F32)
        for y in range(ny):
            lanes = pl.ds(y * nx, nx)
            cell = pl.ds((z * ny + y) * nx, nx)
            back = (right(res[pl.ds(0, cone), lanes], lane1) + res[pl.ds(cone, cone), lanes]
                    + left(res[pl.ds(2 * cone, cone), lanes], lane1))
            slope = (back * d_one[:, cell]).astype(BF16)
            slf = slope.astype(F32)
            slope31[pl.ds(0, cone), cell] = left(slf, lane1).astype(BF16)
            slope31[pl.ds(cone, cone), cell] = slope
            slope31[pl.ds(2 * cone, cone), cell] = right(slf, lane1).astype(BF16)

    g1 = lax.dot_general(stack_v[:, pl.ds(2 * plane, cells)].astype(BF16), slope31[...], NT, preferred_element_type=F32)
    g1 = jnp.concatenate([g1, jnp.zeros((72, nx - 3 * cone), F32)], axis=1)
    late = jnp.concatenate([g1, b2row], axis=0).astype(BF16)
    if cut < tail.shape[0]:
        late = jnp.concatenate([tail[cut:], late], axis=0)
    sb[pl.ds(early, halves * nsh - early)] = late.reshape(halves * nsh - early, rows, nx)

    for h in range(halves):
        @pl.loop(max(early - h * nsh, 0), nsh)
        def _(s, h=h):
            @pl.when(s != me)
            def _():
                shard_copy(h, s).start()

    def drain(buf, sem):
        pltpu.make_async_copy(buf, buf, sem).wait()

    def z_copy(h, d):
        return pltpu.make_async_remote_copy(
            src_ref=zsrc.at[h], dst_ref=zb.at[h, zi], send_sem=pzs, recv_sem=pzr.at[h],
            device_id=column(lax.rem(zi + d, nz)), device_id_type=MESH)

    def out_copy(h, d):
        return pltpu.make_async_remote_copy(
            src_ref=gath.at[h * nsh + me], dst_ref=gath.at[h * nsh + me], send_sem=p2s, recv_sem=p2r,
            device_id=peer(lax.rem(me + d, nsh)), device_id_type=MESH)

    for h in range(halves):
        drain(rb.at[h], p1r.at[h])
        total = (sb[h * nsh + me].astype(F32) + jnp.sum(rb[h].astype(F32), axis=0)).astype(BF16)
        zsrc[h] = total
        zb[h, zi] = total
        for d in range(1, nz):
            z_copy(h, d).start()

    feat[...] = feat32[...].reshape(feat.shape).astype(BF16)
    for h in range(halves):
        drain(zb.at[h, pl.ds(0, nz - 1)], pzr.at[h])
        whole = zb[h, 0].astype(F32)
        for k in range(1, nz):
            whole = whole + zb[h, k].astype(F32)
        gath[h * nsh + me] = whole.astype(BF16)

        @pl.loop(1, nsh)
        def _(d, h=h):
            out_copy(h, d).start()

    others = pl.ds(0, halves * (nsh - 1))
    drain(gath.at[others], p2r)
    packed[...] = gath[...].reshape(packed.shape)

    drain(sb.at[others], p1s)
    drain(gath.at[pl.ds(0, halves * (nz - 1))], pzs)
    drain(gath.at[others], p2s)

    for side in range(2):
        for i in range(len(parts)):
            @pl.when(sends(side, parts[i][0]))
            def _(side=side, i=i):
                vol_copy(side, i).wait_send()

        @pl.when(sends(side, 1))
        def _(side=side):
            cot_copy(side).wait_send()


def unpack(feat, packed, feat_o, g1_o, gb1_o, g2_o, gb2_o, g1, gb1, g2, gb2, sem):
    cin, cone, ctwo = g1.shape[1], g2.shape[1], g2.shape[2]
    k2 = 9 * cone
    half = k2 // 2
    base = k2 + half
    first = pltpu.make_async_copy(feat, feat_o, sem.at[0])
    first.start()
    full = packed[...].astype(F32)
    for ab in range(9):
        r = ab * cone
        g2[ab * 3] = full[r:r + cone, 0:ctwo]
        g2[ab * 3 + 1] = full[r:r + cone, ctwo:2 * ctwo]
    tail = jnp.concatenate([full[k2:base, 0:ctwo], full[k2:base, ctwo:2 * ctwo]], axis=0)
    for ab in range(9):
        g2[ab * 3 + 2] = tail[ab * cone:(ab + 1) * cone]
    copies = [first, pltpu.make_async_copy(g2, g2_o, sem.at[1])]
    copies[1].start()
    for ab in range(9):
        for c in range(3):
            g1[ab * 3 + c] = full[base + ab * 8:base + ab * 8 + cin, c * cone:(c + 1) * cone]
    gb1[...] = full[base + 4 * 8 + cin:base + 4 * 8 + cin + 1, cone:2 * cone]
    gb2[...] = full[base + 72:base + 73, ctwo:2 * ctwo]
    for i, (src, dst) in enumerate(((g1, g1_o), (gb1, gb1_o), (gb2, gb2_o))):
        copies.append(pltpu.make_async_copy(src, dst, sem.at[2 + i]))
        copies[-1].start()
    for copy in copies:
        copy.wait()


def per_device(ni, nz, nd, volume, kernel_one, bias_one, kernel_two, bias_two, cotangent):
    _, cin, planes, ny, nx = volume.shape
    cone, ctwo = kernel_one.shape[0], kernel_two.shape[0]
    cells = planes * ny * nx
    total = 27 * cone * ctwo // nx + 80
    nsh = ni * nd
    halves = 2 if total // nsh % 32 == 0 else 1
    rows = total // nsh // halves
    w1 = jnp.transpose(kernel_one, (2, 3, 4, 1, 0)).reshape(27, cin, cone)
    w2 = jnp.transpose(kernel_two, (2, 3, 4, 1, 0)).reshape(27, cone, ctwo)
    vm = pl.BlockSpec(memory_space=pltpu.VMEM)
    hbm = pl.BlockSpec(memory_space=pltpu.HBM)
    dma = pltpu.SemaphoreType.DMA
    feat, packed = pl.pallas_call(
        functools.partial(kernel, ni, nz, nd),
        out_shape=(
            jax.ShapeDtypeStruct((ctwo, planes, ny, nx), BF16),
            jax.ShapeDtypeStruct((total, nx), BF16),
        ),
        in_specs=[hbm] * 6,
        out_specs=[vm] * 2,
        scratch_shapes=[
            pltpu.VMEM((cin, planes, ny, nx), BF16),
            pltpu.VMEM((27, cin, cone), BF16),
            pltpu.VMEM((1, cone), F32),
            pltpu.VMEM((27, cone, ctwo), BF16),
            pltpu.VMEM((1, ctwo), F32),
            pltpu.VMEM((ctwo, planes, ny, nx), BF16),
            pltpu.VMEM((2, cin, 3, ny, nx), BF16),
            pltpu.VMEM((8 * (planes + 6) * ny, nx), F32),
            pltpu.VMEM((72, (planes + 4) * ny * nx), F32),
            pltpu.VMEM((ctwo * planes * ny, nx), F32),
            pltpu.VMEM((cone, cells), F32),
            pltpu.VMEM((9 * cone + 16, cells + 2 * ny * nx), BF16),
            pltpu.VMEM((3 * ctwo, ny * nx), F32),
            pltpu.VMEM((3 * ctwo, cells), BF16),
            pltpu.VMEM((2, ctwo, 1, ny, nx), BF16),
            pltpu.VMEM((ctwo * ny, nx), F32),
            pltpu.VMEM((9 * ctwo, cells), BF16),
            pltpu.VMEM((ctwo * planes * ny, nx), F32),
            pltpu.VMEM((3 * cone, cells), BF16),
            pltpu.VMEM((halves * nsh, rows, nx), BF16),
            pltpu.VMEM((halves, nsh - 1, rows, nx), BF16),
            pltpu.VMEM((halves, nz, rows, nx), BF16),
            pltpu.VMEM((halves, rows, nx), BF16),
            pltpu.VMEM((halves * nsh, rows, nx), BF16),
            dma((6,)),
            dma((2, max(1, len(halo_parts(planes, nd))))), dma((2, max(1, len(halo_parts(planes, nd))))), dma((2,)), dma((2,)),
            dma, dma((halves,)), dma, dma((halves,)), dma, dma,
        ],
        compiler_params=pltpu.CompilerParams(
            collective_id=0, has_side_effects=True, vmem_limit_bytes=48 * 1024 * 1024),
    )(*(
        pltpu.with_memory_space_constraint(x, pltpu.HBM)
        for x in (
            volume.reshape(cin, planes, ny, nx), w1, bias_one.reshape(1, cone), w2,
            bias_two.reshape(1, ctwo), cotangent.reshape(ctwo, planes, ny, nx))
    ))
    shapes = (((ctwo, planes, ny, nx), BF16), ((27, cin, cone), F32), ((1, cone), F32),
              ((27, cone, ctwo), F32), ((1, ctwo), F32))
    feat, g1, gb1, g2, gb2 = pl.pallas_call(
        unpack,
        out_shape=tuple(jax.ShapeDtypeStruct(*x) for x in shapes),
        in_specs=[vm] * 2,
        out_specs=[hbm] * 5,
        scratch_shapes=[pltpu.VMEM(*x) for x in shapes[1:]] + [dma((5,))],
        compiler_params=pltpu.CompilerParams(vmem_limit_bytes=8 * 1024 * 1024),
    )(feat, packed)
    g1 = jnp.transpose(g1.reshape(3, 3, 3, cin, cone), (4, 3, 0, 1, 2))
    g2 = jnp.transpose(g2.reshape(3, 3, 3, cone, ctwo), (4, 3, 0, 1, 2))
    return feat[None], g1, gb1.reshape(cone), g2, gb2.reshape(ctwo)


def solution(mesh):
    nd = mesh.shape["depth"]
    ni = min(INNER, mesh.shape["dp"])
    nz = mesh.shape["dp"] // ni
    return jax.shard_map(
        functools.partial(per_device, ni, nz, nd),
        mesh=mesh,
        in_specs=(
            P("dp", None, "depth", None, None),
            P(),
            P(),
            P(),
            P(),
            P("dp", None, "depth", None, None),
        ),
        out_specs=(P("dp", None, "depth", None, None), P(), P(), P(), P()),
        check_vma=False,
    )
```
